32 devices in a mesh: dp: 2 (over x), seq: 16 (over z, y, core).
Axes of the slice: x: 2, y: 2, z: 4, core: 2. Of those that a mesh axis runs over, the one named last changes fastest.
Arguments:
- pixels: bfloat16 [4096, 768], P(('dp', 'seq')), may hold values from -6 to 6
- mask: int32 [4096], P(('dp', 'seq')), may hold values 0 or 1
- image_count: int32 [2, 6], P('dp'), may hold values from 1 to 1024, 2048 in all within a row
- image_width: int32 [2, 6], P('dp'), may hold values from 4 to 63
- gsd_index: int32 [2, 6], P('dp'), may hold values from 0 to 8
- step: int32 [1], replicated, may hold values from 2 to 20
- master: float32 [17551360], P(('dp', 'seq')), as said below
- moment_one: float32 [17551360], P(('dp', 'seq')), as said below
- moment_two: float32 [17551360], P(('dp', 'seq')), as said below
Outputs:
- new_master: float32 [17551360], P(('dp', 'seq'))
- new_moment_one: float32 [17551360], P(('dp', 'seq'))
- new_moment_two: float32 [17551360], P(('dp', 'seq'))
- loss: float32 [1], replicated
- grad_norm: float32 [1], replicated
The draws below stay inside these ranges and needn't reach their ends.
Inputs may be any that keep to these rules, and one draw needn't show every extreme that they name: master holds each weight drawn by its fan-in, gains near 1. moment_two is positive. moment_one takes both signs.
All inputs are finite; a program needn't handle non-finite values. No bound on the sum of `mask` on one device may be relied on, other than what follows from the above.
Results may differ from the reference program's by a relative error of at most 0.0024.
The reference program's roundings to bfloat16 on the way count: a program that leaves them out, or rounds other values in their place, can miss the bound.
Values may be sent and summed in bfloat16 or wider, within the bound.
A program may use at most 512 MiB of HBM per device.

```python
import math
import jax
import jax.numpy as jnp
import numpy as np
from jax import lax

D = 1024
HEADS = 16
FF = 4096
DD = 512
DHEADS = 16
DFF = 2048
PATCH = 16
PIX = 768
LOWPIX = 192
SEQ_TOK = 2048
TOKENS = 4096
SCENE = 1024
NIMG = 6
P_TOTAL = 17549248
PARAMS = 17551360
N_DP = 2


clip_level = 0.0001


def param_table():
    return [((PIX, D), PIX ** (-0.5), 0), ((D,), 0.3, 0), ((4, D), 0.1, 1), ((D, 3 * D), D ** (-0.5), 0), ((D, D), 4.0 * D ** (-0.5), 0), ((D,), 0.3, 0), ((D, FF), D ** (-0.5), 0), ((FF,), 0.3, 0), ((FF, D), FF ** (-0.5), 0), ((D,), 0.3, 0), ((D, DD), D ** (-0.5), 0), ((DD,), 0.3, 0), ((DD,), 1.0, 0), ((4, DD), 0.1, 1), ((DD, 3 * DD), DD ** (-0.5), 0), ((DD, DD), 4.0 * DD ** (-0.5), 0), ((DD,), 0.3, 0), ((DD, DFF), DD ** (-0.5), 0), ((DFF,), 0.3, 0), ((DFF, DD), DFF ** (-0.5), 0), ((DD,), 0.3, 0), ((DD, PIX), DD ** (-0.5), 0), ((PIX,), 0.3, 0), ((DD, LOWPIX), DD ** (-0.5), 0), ((LOWPIX,), 0.3, 0)]


def unit_noise(key, shape):
    return jax.random.normal(key, shape, jnp.float32)


def draw_master(key, part):
    pieces = []
    for number, entry in enumerate(param_table()):
        shape, spread, gain_rows = entry
        noise = unit_noise(jax.random.fold_in(key, number), shape) * spread
        if gain_rows == 1:
            noise = noise + jnp.array([1.0, 0.0, 1.0, 0.0], jnp.float32)[:, None]
        pieces.append(noise.reshape(-1))
    pieces.append(0.02 * unit_noise(jax.random.fold_in(key, 777), (PARAMS - P_TOTAL,)))
    return jnp.concatenate(pieces)


def draw_moment_one(key, part):
    return unit_noise(jax.random.fold_in(key, 11), (PARAMS,)) * (clip_level / P_TOTAL ** 0.5)


def draw_moment_two(key, part):
    factor = jnp.exp2(jax.random.uniform(jax.random.fold_in(key, 12), (PARAMS,), jnp.float32, 0.0, 2.0))
    return factor * (clip_level * clip_level / P_TOTAL)


def place_ends(values, stream_key, low, top_value):
    longest = values.shape.index(max(values.shape))
    spots = []
    for shift in (0, 1):
        where = [jax.random.randint(jax.random.fold_in(stream_key, axis), (), 0, length) for axis, length in enumerate(values.shape)]
        where[longest] = (where[longest] + shift) % values.shape[longest]
        spots.append(tuple(where))
    return values.at[spots[0]].set(low).at[spots[1]].set(top_value)


def shard_levels(key, shape, split, smallest, high):
    def one(dim, shards_of):
        steps = jax.random.uniform(jax.random.fold_in(jax.random.fold_in(key, 6), dim), (shards_of,), jnp.float32, smallest / len(split), high / len(split))
        return jnp.repeat(jnp.exp(steps), shape[dim] // shards_of).reshape((-1,) + (1,) * (len(shape) - dim - 1))

    level = one(*split[0])
    for cut in split[1:]:
        level = level * one(*cut)
    return level


def length_profile(number_of, total, reach, skew):
    loads = [(1 << 20) // math.isqrt(rank ** skew) + 1 for rank in range(2, number_of + 1)]
    spare, holding = total - reach - (number_of - 1), [1] * (number_of - 1)
    while spare > 0:
        free = [i for i in range(number_of - 1) if holding[i] < reach]
        pool, remaining = sum([loads[i] for i in free]), spare
        for i in free:
            more = min(reach - holding[i], max(1, remaining * loads[i] // pool), spare)
            holding[i] = holding[i] + more
            spare = spare - more
    return np.array([reach] + holding)


def ragged(rng, number_of, total, most, lean):
    if number_of == 2:
        one = jax.random.randint(rng, (), max(1, total - most), min(most, total - 1) + 1)
        return jnp.stack([one, total - one])
    tallies = jnp.asarray(length_profile(number_of, total, most, lean), jnp.int32)
    twos = (number_of - 1) // 2
    source_of, sink = tallies[1:1 + 2 * twos:2], tallies[2:2 + 2 * twos:2]
    room = jnp.minimum(source_of - 1, most - sink)
    passed = jax.random.randint(jax.random.fold_in(rng, 1), (twos,), 0, 1 << 20) % (room + 1)
    tallies = tallies.at[1:1 + 2 * twos:2].set(source_of - passed).at[2:2 + 2 * twos:2].set(sink + passed)
    return tallies[jax.random.permutation(jax.random.fold_in(rng, 2), number_of)]


def bell_draw(rng, extent, scale, bound, cuts=(), held_as=jnp.bfloat16):
    factor_of = shard_levels(rng, extent, cuts, -0.22, 0.18) if cuts else 1.0
    entries = jax.random.normal(rng, extent, jnp.float32) * scale * factor_of
    return jnp.minimum(jnp.maximum(entries, -bound), bound).astype(held_as)


def setup_inputs(seed: int = 0) -> dict:
    key_of = jax.random.split(jax.random.key(seed), 10)
    pixels = bell_draw(key_of[0], (TOKENS, PIX), 1.0, 6.0, ((0, 32),))
    mask = place_ends((jax.random.randint(key_of[1], (TOKENS,), 0, 4) < 3).astype(jnp.int32), jax.random.fold_in(key_of[1], 1), 0, 1)
    image_count = jax.vmap(lambda own: ragged(own, NIMG, SEQ_TOK, SCENE, 2))(jax.random.split(key_of[2], N_DP)).reshape((N_DP, NIMG)).astype(jnp.int32)
    image_width = place_ends(jax.random.randint(key_of[3], (N_DP, NIMG), 4, 64), jax.random.fold_in(key_of[3], 1), 4, 63).astype(jnp.int32)
    gsd_index = place_ends(jax.random.randint(key_of[4], (N_DP, NIMG), 0, 9), jax.random.fold_in(key_of[4], 1), 0, 8).astype(jnp.int32)
    step = jax.random.randint(key_of[5], (1,), 2, 21).astype(jnp.int32)
    master = draw_master(jax.random.fold_in(key_of[9], 71), 0)
    moment_one = draw_moment_one(jax.random.fold_in(key_of[9], 71), 0)
    moment_two = draw_moment_two(jax.random.fold_in(key_of[9], 71), 0)
    return dict(pixels=pixels, mask=mask, image_count=image_count, image_width=image_width, gsd_index=gsd_index, step=step, master=master, moment_one=moment_one, moment_two=moment_two)


clip_level = 0.0001
peak_rate = 0.1
warm_steps = 10.0
decay_rate = 0.05
adam_eps = 1e-12

@jax.custom_vjp
def low(v):
    return lax.optimization_barrier(v.astype(jnp.bfloat16)).astype(jnp.float32)

@jax.custom_vjp
def low_back(v):
    return v

def low_keep(v):
    return (low(v), None)

def low_pass(kept, grad):
    return (grad,)

def back_keep(v):
    return (v, None)

def back_low(kept, grad):
    return (low(grad),)
low.defvjp(low_keep, low_pass)
low_back.defvjp(back_keep, back_low)

def param_shapes():
    return [(PIX, D), (D,), (4, D), (D, 3 * D), (D, D), (D,), (D, FF), (FF,), (FF, D), (D,), (D, DD), (DD,), (DD,), (4, DD), (DD, 3 * DD), (DD, DD), (DD,), (DD, DFF), (DFF,), (DFF, DD), (DD,), (DD, PIX), (PIX,), (DD, LOWPIX), (LOWPIX,)]

def unpack(flat):
    pieces = []
    offset = 0
    for shape in param_shapes():
        length = math.prod(shape)
        pieces.append(lax.slice_in_dim(flat, offset, offset + length).reshape(shape))
        offset += length
    return pieces

def matmul(a, b):
    return jnp.dot(a, b, precision=lax.Precision.HIGHEST, preferred_element_type=jnp.float32)

def layer_norm(x, gain, shift):
    centred = x - lax.optimization_barrier(jnp.mean(x, axis=-1, keepdims=True))
    return centred * lax.rsqrt(lax.optimization_barrier(jnp.mean(centred * centred, axis=-1, keepdims=True)) + 1e-06) * gain + shift

def geometry(counts, widths, ground, places):
    ends = jnp.cumsum(counts).astype(jnp.int32)
    starts = ends - counts
    inside = ((places[:, None] >= starts[None, :]) & (places[:, None] < ends[None, :])).astype(jnp.int32)
    image = lax.optimization_barrier(jnp.sum(inside * jnp.arange(counts.shape[0], dtype=jnp.int32)[None, :], axis=1))
    start = lax.optimization_barrier(jnp.sum(inside * starts[None, :], axis=1))
    width = lax.optimization_barrier(jnp.sum(inside * widths[None, :], axis=1))
    level = lax.optimization_barrier(jnp.sum(inside * ground[None, :], axis=1))
    local = places - start
    row_num = local // width
    col_num = local - row_num * width
    ratio = jnp.exp2(level.astype(jnp.float32) * 0.25)
    return (image, local, row_num.astype(jnp.float32) * ratio, col_num.astype(jnp.float32) * ratio)

def position_code(row_pos, col_pos, width):
    quarter = width // 4
    freqs = jnp.power(10000.0, -jnp.arange(quarter, dtype=jnp.float32) / quarter)
    row_ang = row_pos[:, None] * freqs[None, :]
    col_ang = col_pos[:, None] * freqs[None, :]
    return jnp.concatenate([jnp.sin(row_ang), jnp.cos(row_ang), jnp.sin(col_ang), jnp.cos(col_ang)], axis=1)

def pool_table():
    values = 3 * PATCH * PATCH
    index = jnp.arange(values, dtype=jnp.int32)
    channel = index % 3
    cell = index // 3
    row_num = cell // PATCH
    col_num = cell % PATCH
    target = (row_num // 2 * (PATCH // 2) + col_num // 2) * 3 + channel
    return (target[:, None] == jnp.arange(values // 4, dtype=jnp.int32)[None, :]).astype(jnp.float32) * 0.25

def attention(queries, keys, values, seen, image, heads):
    total, width = queries.shape
    depth = width // heads
    scale = depth ** (-0.5)
    size = 512 if total % 512 == 0 else total
    count = total // size
    key_heads = keys.reshape(total, heads, depth)
    value_heads = values.reshape(total, heads, depth)

    def one(args):
        query_block, query_image = args
        scores = jnp.einsum('qhd,khd->hqk', query_block, key_heads, precision=lax.Precision.HIGHEST) * scale
        scores = low_back(scores)
        allowed = (query_image[:, None] == image[None, :]) & (seen[None, :] > 0)
        scores = jnp.where(allowed[None], scores, -1e+30)
        shifted = jnp.exp(scores - lax.optimization_barrier(jnp.max(scores, axis=-1, keepdims=True)))
        probs = low(shifted / lax.optimization_barrier(jnp.sum(shifted, axis=-1, keepdims=True)))
        return jnp.einsum('hqk,khd->qhd', probs, value_heads, precision=lax.Precision.HIGHEST)
    out = lax.map(jax.checkpoint(one), (queries.reshape(count, size, heads, depth), image.reshape(count, size)))
    return out.reshape(total, width)

def block(x, weights, seen, image, heads):
    norms, qkv_w, out_w, out_b, up_w, up_b, down_w, down_b = weights
    width = x.shape[1]
    normed = low(layer_norm(x, norms[0], norms[1]))
    mixed = low(low_back(matmul(normed, qkv_w)))
    attended = attention(mixed[:, :width], mixed[:, width:2 * width], mixed[:, 2 * width:], seen, image, heads)
    attended = low_back(low(attended))
    resid = x + low_back(matmul(attended, out_w)) + out_b
    normed_two = low(layer_norm(resid, norms[2], norms[3]))
    pre = low_back(matmul(normed_two, up_w)) + up_b
    hidden_act = low(jax.nn.gelu(pre, approximate=False))
    return resid + low_back(matmul(hidden_act, down_w)) + down_b

def group_loss(weights, pix, mask, counts, widths, ground):
    total = pix.shape[0]
    image, local, row_pos, col_pos = geometry(counts, widths, ground, jnp.arange(total, dtype=jnp.int32))
    hidden = ((mask == 1) & (local != 0)).astype(jnp.float32)
    embedded = low_back(matmul(pix, weights[0])) + weights[1] + position_code(row_pos, col_pos, D)
    encoded = block(embedded, weights[2:10], 1.0 - hidden, image, HEADS)
    projected = low_back(matmul(low(encoded), weights[10])) + weights[11]
    dec_in = jnp.where(hidden[:, None] > 0, weights[12][None, :], projected) + position_code(row_pos, col_pos, DD)
    decoded = low(block(dec_in, weights[13:21], jnp.ones_like(hidden), image, DHEADS))
    high = low_back(matmul(decoded, weights[21])) + weights[22]
    low_pred = low_back(matmul(decoded, weights[23])) + weights[24]
    table = pool_table()
    low_target = matmul(pix, table)
    high_target = pix - matmul(low_target, 4.0 * table.T)
    per_patch = lax.optimization_barrier(jnp.mean(jnp.abs(high - high_target), axis=-1)) + lax.optimization_barrier(jnp.mean((low_pred - low_target) ** 2, axis=-1))
    return (jnp.sum(hidden * per_patch), jnp.sum(hidden))

def reference(pixels, mask, image_count, image_width, gsd_index, step, master, moment_one, moment_two):
    weights = unpack(master.astype(jnp.bfloat16).astype(jnp.float32))
    pix_all = pixels.astype(jnp.float32).reshape(N_DP, SEQ_TOK, PIX)
    mask_all = mask.reshape(N_DP, SEQ_TOK)

    def total_loss(params):

        def step_fn(carry, group):
            part_loss, part_count = jax.checkpoint(group_loss)(params, *group)
            return ((carry[0] + part_loss, carry[1] + part_count), None)
        start = (jnp.zeros((), jnp.float32), jnp.zeros((), jnp.float32))
        (loss_sum, count), _ = lax.scan(step_fn, start, (pix_all, mask_all, image_count, image_width, gsd_index))
        return (loss_sum, count)
    loss_sum, back_fn, count = jax.vjp(total_loss, weights, has_aux=True)
    grads, = back_fn(jnp.ones((), jnp.float32))
    flat = jnp.concatenate([g.reshape(-1) for g in grads] + [jnp.zeros((PARAMS - P_TOTAL,), jnp.float32)])
    grad_norm = jnp.sqrt(jnp.sum(flat * flat)) / count
    clipped = flat * (jnp.minimum(1.0, clip_level / grad_norm) / count)
    first = 0.5 * moment_one + 0.5 * clipped
    second = 0.5 * moment_two + 0.5 * clipped * clipped
    step_value = step[0].astype(jnp.float32)
    correction = 1.0 - jnp.power(0.5, step_value)
    rate = peak_rate * jnp.minimum(1.0, step_value / warm_steps)
    new_master = master - rate * (first / correction / (jnp.sqrt(second / correction) + adam_eps) + decay_rate * master)
    return (new_master, first, second, (loss_sum / count).reshape(1), grad_norm.reshape(1))
```

```python
import functools
import math

import jax
import jax.numpy as jnp
from jax import lax
from jax.experimental import pallas as pl
from jax.experimental.pallas import tpu as pltpu
from jax.sharding import PartitionSpec as P

D = 1024
HEADS = 16
FF = 4096
DD = 512
DHEADS = 16
DFF = 2048
PATCH = 16
PIX = 768
LOWPIX = 192


clip_level = 0.0001
peak_rate = 0.1
warm_steps = 10.0
decay_rate = 0.05
adam_eps = 1e-12


def param_shapes():
    return [
        (PIX, D),
        (D,),
        (4, D),
        (D, 3 * D),
        (D, D),
        (D,),
        (D, FF),
        (FF,),
        (FF, D),
        (D,),
        (D, DD),
        (DD,),
        (DD,),
        (4, DD),
        (DD, 3 * DD),
        (DD, DD),
        (DD,),
        (DD, DFF),
        (DFF,),
        (DFF, DD),
        (DD,),
        (DD, PIX),
        (PIX,),
        (DD, LOWPIX),
        (LOWPIX,),
    ]


def unpack(flat):
    pieces = []
    offset = 0
    for shape in param_shapes():
        length = math.prod(shape)
        pieces.append(lax.slice_in_dim(flat, offset, offset + length).reshape(shape))
        offset += length
    return pieces


def matmul(a, b):
    return jnp.dot(a, b, preferred_element_type=jnp.float32)


def outer(a, b):
    return lax.dot_general(a, b, (((0,), (0,)), ((), ())), preferred_element_type=jnp.float32)


def back_mul(a, weight):
    return lax.dot_general(a, weight, (((1,), (1,)), ((), ())), preferred_element_type=jnp.float32)


def layer_norm(x, gain, shift):
    centred = x - jnp.mean(x, axis=-1, keepdims=True)
    return (
        centred * lax.rsqrt(jnp.mean(centred * centred, axis=-1, keepdims=True) + 1e-06) * gain
        + shift
    )


def geometry(counts, widths, ground, places):
    ends = jnp.cumsum(counts)
    starts = ends - counts
    inside = ((places[:, None] >= starts[None, :]) & (places[:, None] < ends[None, :])).astype(
        jnp.int32
    )
    image = jnp.sum(inside * jnp.arange(counts.shape[0], dtype=jnp.int32)[None, :], axis=1)
    start = jnp.sum(inside * starts[None, :], axis=1)
    width = jnp.sum(inside * widths[None, :], axis=1)
    level = jnp.sum(inside * ground[None, :], axis=1)
    local = places - start
    row_num = local // width
    col_num = local - row_num * width
    ratio = jnp.exp2(level.astype(jnp.float32) * 0.25)
    return (image, local, row_num.astype(jnp.float32) * ratio, col_num.astype(jnp.float32) * ratio)


def position_code(row_pos, col_pos, width):
    quarter = width // 4
    freqs = jnp.power(10000.0, -jnp.arange(quarter, dtype=jnp.float32) / quarter)
    row_ang = row_pos[:, None] * freqs[None, :]
    col_ang = col_pos[:, None] * freqs[None, :]
    return jnp.concatenate(
        [jnp.sin(row_ang), jnp.cos(row_ang), jnp.sin(col_ang), jnp.cos(col_ang)], axis=1
    )


def pool_table():
    values = 3 * PATCH * PATCH
    index = jnp.arange(values, dtype=jnp.int32)
    channel = index % 3
    cell = index // 3
    row_num = cell // PATCH
    col_num = cell % PATCH
    target = (row_num // 2 * (PATCH // 2) + col_num // 2) * 3 + channel
    return (target[:, None] == jnp.arange(values // 4, dtype=jnp.int32)[None, :]).astype(
        jnp.float32
    ) * 0.25


MESH = pl.DeviceIdType.MESH
NEG = -1e30
QB = 256
KB = 256


def swap_kernel(n, x_ref, o_ref, send_sem, recv_sem, own_sem):
    me = lax.axis_index("seq")
    barrier = pltpu.get_barrier_semaphore()
    for k in range(1, n):
        pl.semaphore_signal(
            barrier, inc=1, device_id={"seq": lax.rem(me + k, n)}, device_id_type=MESH
        )
    pl.semaphore_wait(barrier, n - 1)
    copies = []
    for k in range(1, n):
        peer = lax.rem(me + k, n)
        copy = pltpu.make_async_remote_copy(
            src_ref=x_ref.at[peer],
            dst_ref=o_ref.at[me],
            send_sem=send_sem.at[k],
            recv_sem=recv_sem.at[k],
            device_id={"seq": peer},
            device_id_type=MESH,
        )
        copy.start()
        copies.append(copy)
    own = pltpu.make_async_copy(x_ref.at[me], o_ref.at[me], own_sem)
    own.start()
    own.wait()
    for copy in copies:
        copy.wait()


def swap(x, collective):
    n = x.shape[0]
    return pl.pallas_call(
        functools.partial(swap_kernel, n),
        out_shape=jax.ShapeDtypeStruct(x.shape, x.dtype),
        in_specs=[pl.BlockSpec(memory_space=pltpu.VMEM)],
        out_specs=pl.BlockSpec(memory_space=pltpu.VMEM),
        scratch_shapes=[
            pltpu.SemaphoreType.DMA((n,)),
            pltpu.SemaphoreType.DMA((n,)),
            pltpu.SemaphoreType.DMA,
        ],
        compiler_params=pltpu.CompilerParams(collective_id=collective, has_side_effects=True),
        name="swap%d" % collective,
    )(x)


def dot_tn(a, b):
    return lax.dot_general(a, b, (((0,), (0,)), ((), ())), preferred_element_type=jnp.float32)


def dot_nt(a, b):
    return lax.dot_general(a, b, (((1,), (1,)), ((), ())), preferred_element_type=jnp.float32)


def spread(x_ref, wide_ref):
    for s in range(x_ref.shape[0]):
        wide_ref[:, s * x_ref.shape[2] : (s + 1) * x_ref.shape[2]] = x_ref[s]


def scores_of(wide_ref, depth, aux, query, kb, first, last, scale):
    keys = wide_ref[2 * depth : 3 * depth + aux, pl.ds(pl.multiple_of(kb * KB, KB), KB)]
    raw = dot_tn(keys, query) * scale
    index = kb * KB + lax.broadcasted_iota(jnp.int32, raw.shape, 0)
    return jnp.where((index >= first) & (index < last), raw, NEG)


def query_of(wide_ref, depth, aux, qb):
    query = wide_ref[0:depth, qb * QB : (qb + 1) * QB]
    if aux:
        ones = (lax.broadcasted_iota(jnp.int32, (aux, QB), 0) == 0).astype(jnp.bfloat16)
        query = jnp.concatenate([query, ones], axis=0)
    return query


def attend_kernel(depth, aux, span_ref, x_ref, first_ref, last_ref, out_ref, full_ref, lse_ref, wide_ref, s_ref):
    total = wide_ref.shape[1]
    scale = depth ** (-0.5)
    tokens = x_ref.shape[2]
    spread(x_ref, wide_ref)
    for qb in range(total // QB):
        at = slice(qb * QB, (qb + 1) * QB)
        query = query_of(wide_ref, depth, aux, qb)
        first, last = first_ref[:, at], last_ref[:, at]
        low, high = span_ref[0, qb], span_ref[1, qb]

        def score(kb, top):
            s = scores_of(wide_ref, depth, aux, query, kb, first, last, scale)
            s_ref[pl.ds(pl.multiple_of(kb * KB, KB), KB), :] = s
            return jnp.maximum(top, jnp.max(s, axis=0, keepdims=True))

        top = lax.fori_loop(low, high, score, jnp.full((1, QB), NEG, jnp.float32))

        def weigh(kb, mass):
            rows = pl.ds(pl.multiple_of(kb * KB, KB), KB)
            p = jnp.exp(s_ref[rows, :] - top)
            s_ref[rows, :] = p
            return mass + jnp.sum(p, axis=0, keepdims=True)

        mass = lax.fori_loop(low, high, weigh, jnp.zeros((1, QB), jnp.float32))
        inverse = 1.0 / mass

        def gather(kb, total_out):
            rows = pl.ds(pl.multiple_of(kb * KB, KB), KB)
            p = (s_ref[rows, :] * inverse).astype(jnp.bfloat16)
            values = wide_ref[depth : 2 * depth, rows]
            return total_out + jnp.dot(values, p, preferred_element_type=jnp.float32)

        out = lax.fori_loop(low, high, gather, jnp.zeros((depth, QB), jnp.float32))
        full_ref[:, at] = out
        lse_ref[:, at] = top + jnp.log(mass)
        for part in range(QB // tokens):
            out_ref[qb * (QB // tokens) + part] = out[:, part * tokens : (part + 1) * tokens].astype(jnp.bfloat16)


def attend_back_kernel(
    depth, aux, span_ref, x_ref, g_ref, first_ref, last_ref, full_ref, lse_ref, out_ref, wide_ref, gwide_ref, dq_ref, dk_ref, dv_ref
):
    total = wide_ref.shape[1]
    scale = depth ** (-0.5)
    tokens = x_ref.shape[2]
    spread(x_ref, wide_ref)
    spread(g_ref, gwide_ref)
    dk_ref[...] = jnp.zeros_like(dk_ref)
    dv_ref[...] = jnp.zeros_like(dv_ref)
    for qb in range(total // QB):
        at = slice(qb * QB, (qb + 1) * QB)
        query = query_of(wide_ref, depth, aux, qb)
        plain = wide_ref[0:depth, at]
        first, last = first_ref[:, at], last_ref[:, at]
        grad = gwide_ref[:, at]
        lse = lse_ref[:, at]
        dterm = jnp.sum(grad.astype(jnp.float32) * full_ref[:, at], axis=0, keepdims=True)
        low, high = span_ref[0, qb], span_ref[1, qb]

        def step(kb, dq):
            rows = pl.ds(pl.multiple_of(kb * KB, KB), KB)
            s = scores_of(wide_ref, depth, aux, query, kb, first, last, scale)
            p = jnp.exp(s - lse)
            dp = dot_tn(wide_ref[depth : 2 * depth, rows], grad)
            ds = (p * (dp - dterm)).astype(jnp.bfloat16)
            dk_ref[:, rows] += dot_nt(plain, ds)
            dv_ref[:, rows] += dot_nt(grad, p.astype(jnp.bfloat16))
            return dq + jnp.dot(wide_ref[2 * depth : 3 * depth, rows], ds, preferred_element_type=jnp.float32)

        dq_ref[:, at] = lax.fori_loop(low, high, step, jnp.zeros((depth, QB), jnp.float32))
    for s in range(x_ref.shape[0]):
        at = slice(s * tokens, (s + 1) * tokens)
        out_ref[s, 0:depth, :] = (dq_ref[:, at] * scale).astype(jnp.bfloat16)
        out_ref[s, depth : 2 * depth, :] = dv_ref[:, at].astype(jnp.bfloat16)
        out_ref[s, 2 * depth : 3 * depth, :] = (dk_ref[:, at] * scale).astype(jnp.bfloat16)


def vmem_specs(count):
    return [pl.BlockSpec(memory_space=pltpu.VMEM)] * count


def attend(x, spans, first, last, depth, aux):
    n, rows, tokens = x.shape
    total = n * tokens
    return pl.pallas_call(
        functools.partial(attend_kernel, depth, aux),
        out_shape=(
            jax.ShapeDtypeStruct((n, depth, tokens), jnp.bfloat16),
            jax.ShapeDtypeStruct((depth, total), jnp.float32),
            jax.ShapeDtypeStruct((1, total), jnp.float32),
        ),
        in_specs=[pl.BlockSpec(memory_space=pltpu.SMEM)] + vmem_specs(3),
        out_specs=tuple(vmem_specs(3)),
        scratch_shapes=[pltpu.VMEM((rows, total), jnp.bfloat16), pltpu.VMEM((total, QB), jnp.float32)],
        name="attend%d" % depth,
    )(spans, x, first, last)


def attend_back(x, grad, spans, first, last, full, lse, depth, aux):
    n, rows, tokens = x.shape
    total = n * tokens
    return pl.pallas_call(
        functools.partial(attend_back_kernel, depth, aux),
        out_shape=jax.ShapeDtypeStruct((n, 3 * depth, tokens), jnp.bfloat16),
        in_specs=[pl.BlockSpec(memory_space=pltpu.SMEM)] + vmem_specs(6),
        out_specs=vmem_specs(1)[0],
        scratch_shapes=[
            pltpu.VMEM((rows, total), jnp.bfloat16),
            pltpu.VMEM((depth, total), jnp.bfloat16),
            pltpu.VMEM((depth, total), jnp.float32),
            pltpu.VMEM((depth, total), jnp.float32),
            pltpu.VMEM((depth, total), jnp.float32),
        ],
        name="attend_back%d" % depth,
    )(spans, x, grad, first, last, full, lse)


def block_forward(x, weights, hide, where, heads, collective):
    norms, qkv_w, out_w, out_b, up_w, up_b, down_w, down_b = weights
    spans, first, last = where
    gains = norms.astype(jnp.float32)
    rows, width = x.shape
    depth = width // heads
    normed = layer_norm(x, gains[0], gains[1]).astype(jnp.bfloat16)
    mixed = lax.dot_general(
        qkv_w, normed, (((0,), (1,)), ((), ())), preferred_element_type=jnp.float32
    ).astype(jnp.bfloat16)
    mixed = mixed.reshape(3, heads, depth, rows)
    pieces = [mixed[0], mixed[2], mixed[1]]
    aux = 0
    if hide is not None:
        aux = 16
        bias = jnp.zeros((heads, aux, rows), jnp.bfloat16).at[:, 0, :].set(hide.astype(jnp.bfloat16))
        pieces.append(bias)
    shared = swap(jnp.concatenate(pieces, axis=1), collective)
    out, full, lse = attend(shared, spans, first, last, depth, aux)
    attended = swap(out, collective + 1).reshape(width, rows)
    resid = x + dot_tn(attended, out_w) + out_b.astype(jnp.float32)
    normed_two = layer_norm(resid, gains[2], gains[3]).astype(jnp.bfloat16)
    pre = matmul(normed_two, up_w) + up_b.astype(jnp.float32)
    hidden_act = jax.nn.gelu(pre, approximate=False).astype(jnp.bfloat16)
    result = resid + matmul(hidden_act, down_w) + down_b.astype(jnp.float32)
    kept = (x, normed, shared, full, lse, attended, resid, normed_two, pre, hidden_act)
    return (result, kept)


def block_backward(grad, weights, kept, where, heads, collective):
    norms, qkv_w, out_w, out_b, up_w, up_b, down_w, down_b = weights
    spans, first, last = where
    gains = norms.astype(jnp.float32)
    x, normed, shared, full, lse, attended, resid, normed_two, pre, hidden_act = kept
    rows, width = x.shape
    depth = width // heads
    aux = shared.shape[1] - 3 * depth
    grad_low = grad.astype(jnp.bfloat16)
    grad_down = outer(hidden_act, grad_low)
    grad_down_b = jnp.sum(grad, axis=0)
    _, gelu_back = jax.vjp(lambda value: jax.nn.gelu(value, approximate=False), pre)
    (grad_pre,) = gelu_back(back_mul(grad_low, down_w))
    pre_low = grad_pre.astype(jnp.bfloat16)
    grad_up = outer(normed_two, pre_low)
    grad_up_b = jnp.sum(grad_pre, axis=0)
    _, norm_two_back = jax.vjp(layer_norm, resid, gains[2], gains[3])
    grad_resid, grad_gain_two, grad_shift_two = norm_two_back(back_mul(pre_low, up_w))
    grad_resid = grad_resid + grad
    resid_low = grad_resid.astype(jnp.bfloat16)
    grad_out = matmul(attended, resid_low)
    grad_out_b = jnp.sum(grad_resid, axis=0)
    grad_attended = back_mul(out_w, resid_low).astype(jnp.bfloat16)
    grad_attended = swap(grad_attended.reshape(heads, depth, rows), collective + 1)
    back = attend_back(shared, grad_attended, spans, first, last, full, lse, depth, aux)
    back = swap(back, collective + 2).reshape(heads, 3, depth, rows)
    mixed_low = jnp.stack([back[:, 0], back[:, 2], back[:, 1]]).reshape(3 * width, rows)
    grad_qkv = lax.dot_general(
        normed, mixed_low, (((0,), (1,)), ((), ())), preferred_element_type=jnp.float32
    )
    _, norm_one_back = jax.vjp(layer_norm, x, gains[0], gains[1])
    grad_x, grad_gain_one, grad_shift_one = norm_one_back(
        lax.dot_general(mixed_low, qkv_w, (((0,), (1,)), ((), ())), preferred_element_type=jnp.float32)
    )
    grad_norms = jnp.stack([grad_gain_one, grad_shift_one, grad_gain_two, grad_shift_two])
    return (
        grad_x + grad_resid,
        [grad_norms, grad_qkv, grad_out, grad_out_b, grad_up, grad_up_b, grad_down, grad_down_b],
    )


def reach(counts, total):
    ends = jnp.cumsum(counts)
    starts = ends - counts
    places = jnp.arange(total, dtype=jnp.int32)
    inside = ((places[:, None] >= starts[None, :]) & (places[:, None] < ends[None, :])).astype(jnp.int32)
    first = jnp.sum(inside * starts[None, :], axis=1)
    last = jnp.sum(inside * ends[None, :], axis=1)
    low = first[::QB] // KB
    high = (last[QB - 1 :: QB] + KB - 1) // KB
    return (jnp.stack([low, high]), first[None, :], last[None, :])


def body(pixels, mask, image_count, image_width, gsd_index, step, master, moment_one, moment_two):
    flat = lax.all_gather(master.astype(jnp.bfloat16), ("dp", "seq"), axis=0, tiled=True)
    weights = unpack(flat)
    rows = pixels.shape[0]
    group_rows = rows * lax.axis_size("seq")
    places = lax.axis_index("seq") * rows + jnp.arange(rows, dtype=jnp.int32)
    counts, widths, ground = (image_count[0], image_width[0], gsd_index[0])
    _, local, row_pos, col_pos = geometry(counts, widths, ground, places)
    where = reach(counts, group_rows)
    hidden = ((mask == 1) & (local != 0)).astype(jnp.float32)
    count_local = jnp.sum(hidden)
    count = lax.psum(count_local, ("dp", "seq"))
    embedded = (
        matmul(pixels, weights[0])
        + weights[1].astype(jnp.float32)
        + position_code(row_pos, col_pos, D)
    )
    encoded, enc_kept = block_forward(
        embedded, weights[2:10], hidden * NEG, where, HEADS, 0
    )
    encoded_low = encoded.astype(jnp.bfloat16)
    projected = matmul(encoded_low, weights[10]) + weights[11].astype(jnp.float32)
    dec_in = jnp.where(
        hidden[:, None] > 0, weights[12].astype(jnp.float32)[None, :], projected
    ) + position_code(row_pos, col_pos, DD)
    decoded, dec_kept = block_forward(
        dec_in, weights[13:21], None, where, DHEADS, 3
    )
    decoded_low = decoded.astype(jnp.bfloat16)
    high = matmul(decoded_low, weights[21]) + weights[22].astype(jnp.float32)
    low_pred = matmul(decoded_low, weights[23]) + weights[24].astype(jnp.float32)
    table = pool_table()
    pix_wide = pixels.astype(jnp.float32)
    low_target = jnp.dot(
        pix_wide, table, precision=lax.Precision.HIGHEST, preferred_element_type=jnp.float32
    )
    high_target = pix_wide - jnp.dot(
        low_target,
        4.0 * table.T,
        precision=lax.Precision.HIGHEST,
        preferred_element_type=jnp.float32,
    )
    per_patch = jnp.mean(jnp.abs(high - high_target), axis=-1) + jnp.mean(
        (low_pred - low_target) ** 2, axis=-1
    )
    loss_local = jnp.sum(hidden * per_patch)
    grad_high = hidden[:, None] * jnp.sign(high - high_target) / PIX
    grad_low_pred = hidden[:, None] * 2.0 * (low_pred - low_target) / LOWPIX
    high_low = grad_high.astype(jnp.bfloat16)
    lowband_low = grad_low_pred.astype(jnp.bfloat16)
    grad_decoded = back_mul(high_low, weights[21]) + back_mul(lowband_low, weights[23])
    grad_dec_in, dec_grads = block_backward(
        grad_decoded, weights[13:21], dec_kept, where, DHEADS, 3
    )
    grad_token = jnp.sum(hidden[:, None] * grad_dec_in, axis=0)
    grad_projected = grad_dec_in * (1.0 - hidden)[:, None]
    projected_low = grad_projected.astype(jnp.bfloat16)
    grad_encoded = back_mul(projected_low, weights[10])
    grad_embedded, enc_grads = block_backward(
        grad_encoded, weights[2:10], enc_kept, where, HEADS, 0
    )
    grads = (
        [outer(pixels, grad_embedded.astype(jnp.bfloat16)), jnp.sum(grad_embedded, axis=0)]
        + enc_grads
        + [outer(encoded_low, projected_low), jnp.sum(grad_projected, axis=0), grad_token]
        + dec_grads
        + [
            outer(decoded_low, high_low),
            jnp.sum(grad_high, axis=0),
            outer(decoded_low, lowband_low),
            jnp.sum(grad_low_pred, axis=0),
        ]
    )
    shard = master.shape[0]
    groups, seqs = (lax.axis_size("dp"), lax.axis_size("seq"))
    total_params = shard * groups * seqs
    used = sum((math.prod(shape) for shape in param_shapes()))
    grad_flat = jnp.concatenate(
        [g.reshape(-1) for g in grads] + [jnp.zeros((total_params - used,), jnp.float32)]
    )
    partial_share = lax.psum_scatter(
        grad_flat.reshape(groups, seqs, shard), "seq", scatter_dimension=1, tiled=True
    )
    summed = lax.psum(partial_share, "dp")
    owned = lax.dynamic_index_in_dim(summed, lax.axis_index("dp"), 0, keepdims=False)[0]
    square_sum = jnp.sum(owned * owned)
    loss_total, square_total = lax.psum((loss_local, square_sum), ("dp", "seq"))
    grad_norm = jnp.sqrt(square_total) / count
    clipped = owned * (jnp.minimum(1.0, clip_level / grad_norm) / count)
    first = 0.5 * moment_one + 0.5 * clipped
    second = 0.5 * moment_two + 0.5 * clipped * clipped
    step_value = step[0].astype(jnp.float32)
    correction = 1.0 - jnp.power(0.5, step_value)
    rate = peak_rate * jnp.minimum(1.0, step_value / warm_steps)
    new_master = master - rate * (
        first / correction / (jnp.sqrt(second / correction) + adam_eps) + decay_rate * master
    )
    return (new_master, first, second, (loss_total / count).reshape(1), grad_norm.reshape(1))


def solution(mesh):
    in_specs = (
        P(("dp", "seq"), None),
        P(("dp", "seq")),
        P("dp", None),
        P("dp", None),
        P("dp", None),
        P(),
        P(("dp", "seq")),
        P(("dp", "seq")),
        P(("dp", "seq")),
    )
    out_specs = (P(("dp", "seq")), P(("dp", "seq")), P(("dp", "seq")), P(), P())
    return jax.shard_map(body, mesh=mesh, in_specs=in_specs, out_specs=out_specs, check_vma=False)
```
